32 devices in a mesh: row: 4 (over y, core), col: 8 (over z, x).
Axes of the slice: x: 2, y: 2, z: 4, core: 2. Of those that a mesh axis runs over, the one named last changes fastest.
Arguments:
- covariance: float32 [16384, 16384], P('row', 'col'), as said below
- weights: float32 [16384], P(('row', 'col')), may hold values from 0.5 to 1
- dual_slacks: float32 [16384], P(('row', 'col')), may hold values from 2.5 to 10
- returns: float32 [16384], P(('row', 'col')), may hold values from -6 to 6
- targets: float32 [256], P('col'), may hold values from 0.5 to 1
- sector_duals: float32 [256], replicated, may hold values from -6 to 6
- lengths: int32 [256], replicated, may hold values from 1 to 1024, 16384 in all
Outputs:
- factored: float32 [16384, 16384], P('row', 'col')
- solved_rhs: float32 [16384], P('row')
- sector_cols: float32 [16384, 256], P('row', 'col')
- sector_resid: float32 [256], P('col')
The draws below stay inside these ranges and needn't reach their ends.
Inputs may be any that keep to these rules, and one draw needn't show every extreme that they name: `lengths`: lengths sum to 16384. `covariance`: only the lower triangle with the diagonal is read; with the added diagonal the system is positive definite.
All inputs are finite; a program needn't handle non-finite values.
Results may differ from the reference program's by a relative error of at most 0.0003.
Values sent between devices are 32-bit elements; how exact they have to be, the bound alone decides.
A program may use at most 192 MiB of HBM per device.

```python
import math
import jax
import jax.numpy as jnp
import numpy as np
from jax import lax

N = 16384
SECT = 256
MOST_LEN = 1024
NB = 128
PANELS = 8


def draw_covariance(key, part):
    factor_count = max(4, min(64, N // 32))
    key_load, key_beta, key_noise = jax.random.split(key, 3)
    loadings = jnp.clip(jax.random.normal(key_load, (N, factor_count), jnp.float32), -4.0, 4.0)
    noise = jnp.clip(jax.random.normal(key_noise, (N, N), jnp.float32), -4.0, 4.0)
    market = 1.0
    betas = jax.random.uniform(key_beta, (N,), jnp.float32, 0.5, 1.5)
    scaled = loadings
    factor_part = jnp.dot(scaled, scaled.T, precision=lax.Precision.HIGHEST) * (0.5 / factor_count)
    market_part = market / N * betas[:, None] * betas[None, :]
    return factor_part + market_part + noise * (1.0 / math.sqrt(N))


def levels(rng, dims, pieces, smallest, high):
    factor_of, own = 1.0, jax.random.fold_in(rng, 6)
    for position, shards_of in pieces:
        steps = jnp.exp(jax.random.uniform(jax.random.fold_in(own, position), (shards_of,), jnp.float32, smallest / len(pieces), high / len(pieces)))
        factor_of = factor_of * jnp.repeat(steps, dims[position] // shards_of).reshape([-1 if axis == position else 1 for axis in range(len(dims))])
    return factor_of


def profile(count, total, reach, slope):
    loads = [(1 << 20) // math.isqrt(standing ** slope) + 1 for standing in range(2, count + 1)]
    spare, counts = total - reach - (count - 1), [1] * (count - 1)
    while spare > 0:
        candidates = [i for i in range(count - 1) if counts[i] < reach]
        mass, left = sum([loads[i] for i in candidates]), spare
        for i in candidates:
            more = min(reach - counts[i], max(1, left * loads[i] // mass), spare)
            counts[i] = counts[i] + more
            spare = spare - more
    return np.array([reach] + counts)


def uneven_parts(key, amount, total, most, skew):
    if amount == 2:
        one = jax.random.randint(key, (), max(1, total - most), min(most, total - 1) + 1)
        return jnp.stack([one, total - one])
    sizes = jnp.asarray(profile(amount, total, most, skew), jnp.int32)
    couples = (amount - 1) // 2
    giver, receiver = sizes[1:1 + 2 * couples:2], sizes[2:2 + 2 * couples:2]
    margin = jnp.minimum(giver - 1, most - receiver)
    moved = jax.random.randint(jax.random.fold_in(key, 1), (couples,), 0, 1 << 20) % (margin + 1)
    sizes = sizes.at[1:1 + 2 * couples:2].set(giver - moved).at[2:2 + 2 * couples:2].set(receiver + moved)
    return sizes[jax.random.permutation(jax.random.fold_in(key, 2), amount)]


def centred(stream_key, shape, spread, reach, cuts=(), held_as=jnp.bfloat16):
    gain = levels(stream_key, shape, cuts, -0.22, 0.18) if cuts else 1.0
    entries = jax.random.normal(stream_key, shape, jnp.float32) * spread * gain
    return jnp.minimum(jnp.maximum(entries, -reach), reach).astype(held_as)


def setup_inputs(seed: int = 0) -> dict:
    key_of = jax.random.split(jax.random.key(seed), 8)
    covariance = draw_covariance(jax.random.fold_in(key_of[7], 71), 0)
    weights = jnp.clip(jnp.exp(math.log(1.0) - 0.6931472 * jax.random.uniform(key_of[1], (N,), jnp.float32) ** levels(key_of[1], (N,), ((0, 32),), -0.2, 0.2)), 0.5, 1.0)
    dual_slacks = jnp.clip(jnp.exp(math.log(10.0) - 1.3862944 * jax.random.uniform(key_of[2], (N,), jnp.float32) ** levels(key_of[2], (N,), ((0, 32),), -0.2, 0.2)), 2.5, 10.0)
    returns = centred(key_of[3], (N,), 1.0, 6.0, ((0, 32),), jnp.float32)
    targets = jnp.clip(0.5 + 0.5 * jax.random.uniform(key_of[4], (SECT,), jnp.float32) ** levels(key_of[4], (SECT,), ((0, 8),), -0.2, 0.2), 0.5, 1.0)
    sector_duals = centred(key_of[5], (SECT,), 1.0, 6.0, (), jnp.float32)
    lengths = uneven_parts(key_of[6], SECT, N, MOST_LEN, 2).astype(jnp.int32)
    return dict(covariance=covariance, weights=weights, dual_slacks=dual_slacks, returns=returns, targets=targets, sector_duals=sector_duals, lengths=lengths)


HIGH = lax.Precision.HIGHEST
SIGMA_GAP = 0.5

def symmetric_product(covariance, weights):
    blocks = 16
    rows_per = covariance.shape[0] // blocks
    stacked = covariance.reshape(blocks, rows_per, covariance.shape[1])
    columns = jnp.arange(covariance.shape[1], dtype=jnp.int32)
    starts = jnp.arange(blocks, dtype=jnp.int32) * rows_per

    def accumulate(column_sum, item):
        tile_block, start_row = item
        row_index = start_row + jnp.arange(rows_per, dtype=jnp.int32)
        lower_part = jnp.where(row_index[:, None] >= columns[None, :], tile_block, 0.0)
        strict = jnp.where(row_index[:, None] > columns[None, :], tile_block, 0.0)
        weight_rows = lax.dynamic_slice_in_dim(weights, start_row, rows_per)
        column_sum = column_sum + jnp.dot(weight_rows, strict, precision=HIGH)
        return (column_sum, jnp.dot(lower_part, weights, precision=HIGH))
    column_sum, row_parts = lax.scan(accumulate, jnp.zeros((covariance.shape[1],), jnp.float32), (stacked, starts))
    return column_sum + row_parts.reshape(-1)

def reference(covariance, weights, dual_slacks, returns, targets, sector_duals, lengths):
    sector_ends = jnp.cumsum(lengths).astype(jnp.int32)
    offsets = sector_ends - lengths
    assets = jnp.arange(N, dtype=jnp.int32)
    member = ((assets[:, None] >= offsets[None, :]) & (assets[:, None] < sector_ends[None, :])).astype(jnp.float32)
    sector_sizes = lengths.astype(jnp.float32)
    sector_resid = targets - jnp.dot(weights, member, precision=HIGH) / sector_sizes
    mean_gap = jnp.sum(weights * dual_slacks) / N
    product = symmetric_product(covariance, weights)
    prices = jnp.dot(member, sector_duals, precision=HIGH)
    rhs = returns - product - prices + SIGMA_GAP * mean_gap / weights
    extras = jnp.concatenate([rhs[:, None], member / jnp.sqrt(sector_sizes)[None, :]], axis=1)
    split = PANELS * NB
    diag_term = dual_slacks / weights
    head = covariance[:split, :split]
    head_index = jnp.arange(split, dtype=jnp.int32)
    head_lower = jnp.tril(head).at[head_index, head_index].add(diag_term[:split])
    head_sym = head_lower + jnp.tril(head, -1).T
    factor_head = jnp.linalg.cholesky(head_sym)
    inverse_head = lax.linalg.triangular_solve(factor_head, jnp.eye(split, dtype=jnp.float32), left_side=True, lower=True)
    factor_tail = jnp.dot(covariance[split:, :split], inverse_head.T, precision=HIGH)
    tail_index = jnp.arange(N - split, dtype=jnp.int32)
    schur = covariance[split:, split:] - jnp.dot(factor_tail, factor_tail.T, precision=HIGH)
    schur = schur.at[tail_index, tail_index].add(diag_term[split:])
    solved_head = jnp.dot(inverse_head, extras[:split], precision=HIGH)
    solved_tail = extras[split:] - jnp.dot(factor_tail, solved_head, precision=HIGH)
    top = jnp.concatenate([jnp.tril(factor_head), jnp.zeros((split, N - split), jnp.float32)], axis=1)
    bottom = jnp.concatenate([factor_tail, jnp.tril(schur)], axis=1)
    factored = jnp.concatenate([top, bottom], axis=0)
    solved = jnp.concatenate([solved_head, solved_tail], axis=0)
    return (factored, solved[:, 0], solved[:, 1:], sector_resid)
```

```python
import jax
import jax.numpy as jnp
from jax import lax
from jax.experimental import pallas as pl
from jax.experimental.pallas import tpu as pltpu
from jax.sharding import PartitionSpec as P

NB = 128
PANELS = 8


HIGHEST = lax.Precision.HIGHEST
HIGH = lax.Precision.HIGH
SIGMA_GAP = 0.5
NT = (((1,), (1,)), ((), ()))


def eliminate(block):
    width = block.shape[0]
    rows = lax.broadcasted_iota(jnp.int32, (width, width), 0)
    lanes = lax.broadcasted_iota(jnp.int32, (width, width), 1)

    def step(j, carry):
        left, right = carry
        at_row = rows == j
        row = jnp.sum(jnp.where(at_row, left, 0.0), axis=0, keepdims=True)
        other = jnp.sum(jnp.where(at_row, right, 0.0), axis=0, keepdims=True)
        column = jnp.sum(jnp.where(lanes == j, left, 0.0), axis=1, keepdims=True)
        pivot = jnp.sum(jnp.where(lanes[:1] == j, row, 0.0), axis=1, keepdims=True)
        scale = lax.rsqrt(pivot)
        scale = scale * (1.5 - 0.5 * pivot * scale * scale)
        row = row * scale
        other = other * scale
        column = column * scale
        below = rows > j
        left = jnp.where(below, left - column * row, jnp.where(at_row, row, left))
        right = jnp.where(below, right - column * other, jnp.where(at_row, other, right))
        return (left, right)

    identity = (rows == lanes).astype(jnp.float32)
    upper, inverse = lax.fori_loop(0, width, step, (block, identity))
    upper = jnp.where(lanes >= rows, upper, 0.0)
    return (upper.T, inverse)


def factor_kernel(head_ref, factor_ref, inverse_ref):
    order = head_ref.shape[0]
    factor_ref[...] = head_ref[...]
    inverse_ref[...] = jnp.zeros_like(inverse_ref)
    for first in range(0, order, NB):
        last = first + NB
        here = slice(first, last)
        lower, inverse = eliminate(factor_ref[here, here])
        factor_ref[here, here] = lower
        inverse_ref[here, here] = inverse
        if first:
            done = jnp.dot(
                factor_ref[here, :first],
                inverse_ref[:first, :first],
                precision=HIGHEST,
                preferred_element_type=jnp.float32,
            )
            inverse_ref[here, :first] = -jnp.dot(
                inverse, done, precision=HIGHEST, preferred_element_type=jnp.float32
            )
        if last < order:
            below = lax.dot_general(
                factor_ref[last:, here], inverse, NT, precision=HIGHEST,
                preferred_element_type=jnp.float32,
            )
            factor_ref[last:, here] = below
            factor_ref[here, last:] = jnp.zeros((NB, order - last), jnp.float32)
            for top in range(last, order, NB):
                factor_ref[top:, top:top + NB] -= lax.dot_general(
                    below[top - last:], below[top - last:top - last + NB], NT,
                    precision=HIGHEST, preferred_element_type=jnp.float32,
                )


def lower_inverse(symmetric):
    order = symmetric.shape[0]
    shape = jax.ShapeDtypeStruct((order, order), jnp.float32)
    return pl.pallas_call(
        factor_kernel,
        out_shape=(shape, shape),
        in_specs=[pl.BlockSpec(memory_space=pltpu.VMEM)],
        out_specs=(pl.BlockSpec(memory_space=pltpu.VMEM),) * 2,
        compiler_params=pltpu.CompilerParams(vmem_limit_bytes=48 * 1024 * 1024),
        cost_estimate=pl.CostEstimate(
            flops=200 * order**3, bytes_accessed=12 * order * order, transcendentals=order
        ),
    )(symmetric)


def on_device(covariance, weights, dual_slacks, returns, targets, sector_duals, lengths):
    tile_rows, tile_cols = covariance.shape
    row_devices, col_devices = lax.axis_size("row"), lax.axis_size("col")
    order_total = tile_rows * row_devices
    row_id = lax.axis_index("row")
    col_id = lax.axis_index("col")
    row_start = row_id * tile_rows
    col_start = col_id * tile_cols
    sectors_here = targets.shape[0]
    lead = PANELS * NB
    piece = tile_rows // col_devices

    head_raw = jnp.where((row_id == 0) & (col_id == 0), covariance[:lead, :lead], 0.0)
    head_raw = lax.psum(head_raw, ("row", "col"))
    lead_raw = jnp.where(col_id == 0, covariance[:, :lead], 0.0)
    lead_raw = lax.psum_scatter(lead_raw, "col", scatter_dimension=0, tiled=True)

    stacked = jnp.stack([weights, dual_slacks, returns])
    full = lax.all_gather(stacked, ("row", "col"), axis=1, tiled=True)
    full_weights, full_slacks, full_returns = full[0], full[1], full[2]
    full_diag = full_slacks / full_weights

    head = jnp.tril(head_raw)
    symmetric = head + jnp.tril(head_raw, -1).T
    eye = jnp.arange(lead)[:, None] == jnp.arange(lead)[None, :]
    symmetric = symmetric + jnp.where(eye, full_diag[:lead, None], 0.0)
    factor, inverse = lower_inverse(symmetric)

    mine = lax.dot_general(lead_raw, inverse, NT, precision=HIGH)
    piece_id = row_id * col_devices + col_id
    piece_start = piece_id * piece
    padded = jnp.pad(factor, ((0, max(0, piece - lead % piece) if lead % piece else 0), (0, 0)))
    head_rows = lax.dynamic_slice_in_dim(
        padded, jnp.minimum(piece_start, padded.shape[0] - piece), piece
    )
    piece_index = piece_start + jnp.arange(piece, dtype=jnp.int32)
    mine = jnp.where((piece_index < lead)[:, None], head_rows, mine)
    count = row_devices * col_devices
    moves = []
    for source in range(count):
        target_row, target_col = source % row_devices, source // row_devices
        moves.append((source, target_row * col_devices + target_col))
    moved = lax.ppermute(mine, ("row", "col"), moves)
    cols_factor = lax.all_gather(moved, "row", axis=0, tiled=True)
    rows_factor = lax.all_gather(mine, "col", axis=0, tiled=True)

    sector_ends = jnp.cumsum(lengths)
    offsets = sector_ends - lengths
    mean_gap = jnp.sum(full_weights * full_slacks) / order_total
    sector_first = col_id * sectors_here
    local_offsets = lax.dynamic_slice_in_dim(offsets, sector_first, sectors_here)
    local_ends = lax.dynamic_slice_in_dim(sector_ends, sector_first, sectors_here)
    sector_sizes = lax.dynamic_slice_in_dim(lengths, sector_first, sectors_here).astype(jnp.float32)
    all_assets = jnp.arange(order_total, dtype=jnp.int32)
    column_member = (all_assets[None, :] >= local_offsets[:, None]) & (
        all_assets[None, :] < local_ends[:, None]
    )
    held = jnp.sum(jnp.where(column_member, full_weights[None, :], 0.0), axis=1)
    sector_resid = targets - held / sector_sizes

    global_rows = row_start + jnp.arange(tile_rows, dtype=jnp.int32)
    global_cols = col_start + jnp.arange(tile_cols, dtype=jnp.int32)
    lower_mask = global_rows[:, None] >= global_cols[None, :]
    strict_mask = global_rows[:, None] > global_cols[None, :]
    weight_rows = lax.dynamic_slice_in_dim(full_weights, row_start, tile_rows)
    weight_cols = lax.dynamic_slice_in_dim(full_weights, col_start, tile_cols)
    row_part = jnp.sum(jnp.where(lower_mask, covariance * weight_cols[None, :], 0.0), axis=1)
    col_part = jnp.sum(jnp.where(strict_mask, covariance * weight_rows[:, None], 0.0), axis=0)
    zeros = jnp.zeros((order_total,), jnp.float32)
    partial_value = lax.dynamic_update_slice_in_dim(
        zeros, row_part, row_start, 0
    ) + lax.dynamic_update_slice_in_dim(zeros, col_part, col_start, 0)
    partial_value, symmetric = lax.optimization_barrier((partial_value, symmetric))
    product = lax.psum(partial_value, ("row", "col"))

    def right_sides(start, size):
        index = start + jnp.arange(size, dtype=jnp.int32)
        cut = lambda value: lax.dynamic_slice_in_dim(value, start, size)
        member = (index[:, None] >= offsets[None, :]) & (index[:, None] < sector_ends[None, :])
        prices = jnp.sum(jnp.where(member, sector_duals[None, :], 0.0), axis=1)
        rhs = cut(full_returns) - cut(product) - prices + SIGMA_GAP * mean_gap / cut(full_weights)
        local = (index[:, None] >= local_offsets[None, :]) & (index[:, None] < local_ends[None, :])
        columns = local.astype(jnp.float32) * lax.rsqrt(sector_sizes)[None, :]
        return jnp.concatenate([rhs[:, None], columns], axis=1)

    solved_head = jnp.dot(inverse, right_sides(0, lead), precision=HIGHEST)
    extras = right_sides(row_start, tile_rows)

    update = lax.dot_general(rows_factor, cols_factor, NT, precision=HIGH)
    diag_rows = lax.dynamic_slice_in_dim(full_diag, row_start, tile_rows)
    on_diagonal = global_rows[:, None] == global_cols[None, :]
    work = covariance - update + jnp.where(on_diagonal, diag_rows[:, None], 0.0)
    lead_part = jnp.pad(rows_factor, ((0, 0), (0, tile_cols - lead)))
    work = jnp.where((global_cols < lead)[None, :], lead_part, work)
    factored = jnp.where(lower_mask, work, 0.0)

    extras = extras - jnp.dot(rows_factor, solved_head, precision=HIGHEST)
    top = jnp.where(row_id == 0, solved_head, extras[:lead])
    extras = lax.dynamic_update_slice_in_dim(extras, top, 0, 0)
    return (factored, extras[:, 0], extras[:, 1:], sector_resid)


def solution(mesh):
    return jax.shard_map(
        on_device,
        mesh=mesh,
        in_specs=(
            P("row", "col"),
            P(("row", "col")),
            P(("row", "col")),
            P(("row", "col")),
            P("col"),
            P(),
            P(),
        ),
        out_specs=(P("row", "col"), P("row"), P("row", "col"), P("col")),
        check_vma=False,
    )
```
